32 devices in a mesh: rep: 8 (over y, x, core), shard: 4 (over z).
Axes of the slice: x: 2, y: 2, z: 4, core: 2. Of those that a mesh axis runs over, the one named last changes fastest.
Arguments:
- tokens: bfloat16 [512, 32, 768], P(None, ('rep', 'shard')), may hold values from -6 to 6
- cotangent: bfloat16 [512, 32, 768], P(None, ('rep', 'shard')), may hold values from -6 to 6
- lengths: int32 [128], replicated, may hold values from 0 to 512, as said below
- packing: int32 [128], replicated, may hold values from 0 to 127, as said below
- qkv_weight: bfloat16 [768, 2304], P('shard'), may hold values from -0.21875 to 0.21875
- query_bias: bfloat16 [768], P('shard'), may hold values from -3 to 3
- value_bias: bfloat16 [768], P('shard'), may hold values from -0.29882812 to 0.29882812
- out_weight: bfloat16 [768, 768], P('shard'), may hold values from -1.75 to 1.75
- out_bias: bfloat16 [768], P('shard'), may hold values from -1.1953125 to 1.1953125
- first_gain: bfloat16 [768], P('shard'), may hold values from 0.5 to 1.5
- first_shift: bfloat16 [768], P('shard'), may hold values from -1.1953125 to 1.1953125
- up_weight: bfloat16 [768, 3072], P('shard'), may hold values from -0.21875 to 0.21875
- up_bias: bfloat16 [3072], P('shard'), may hold values from -1.1953125 to 1.1953125
- down_weight: bfloat16 [3072, 768], P('shard'), may hold values from -0.109375 to 0.109375
- down_bias: bfloat16 [768], P('shard'), may hold values from -1.1953125 to 1.1953125
- second_gain: bfloat16 [768], P('shard'), may hold values from 0.5 to 1.5
- second_shift: bfloat16 [768], P('shard'), may hold values from -1.1953125 to 1.1953125
Outputs:
- output: bfloat16 [512, 32, 768], P(None, ('rep', 'shard'))
- grad_tokens: bfloat16 [512, 32, 768], P(None, ('rep', 'shard'))
- grad_qkv_weight: float32 [768, 2304], P('shard')
- grad_query_bias: float32 [768], P('shard')
- grad_value_bias: float32 [768], P('shard')
- grad_out_weight: float32 [768, 768], P('shard')
- grad_out_bias: float32 [768], P('shard')
- grad_first_gain: float32 [768], P('shard')
- grad_first_shift: float32 [768], P('shard')
- grad_up_weight: float32 [768, 3072], P('shard')
- grad_up_bias: float32 [3072], P('shard')
- grad_down_weight: float32 [3072, 768], P('shard')
- grad_down_bias: float32 [768], P('shard')
- grad_second_gain: float32 [768], P('shard')
- grad_second_shift: float32 [768], P('shard')
The draws below stay inside these ranges and needn't reach their ends.
Inputs may be any that keep to these rules, and one draw needn't show every extreme that they name: lengths[s] counts the tokens of sequence s; 0 marks an unused entry. A used sequence's length is more than its span less 128 / 2. The spans of the sequences that packing puts in one slot add up to exactly 512. A permutation of 0 to 127; sequence s goes to slot packing[s] // 4 as its entry packing[s] % 4.
All inputs are finite; a program needn't handle non-finite values.
Results may differ from the reference program's by a relative error of at most 0.015.
Values may be sent and summed in bfloat16 or wider, within the bound.
No kernel may reach another device: no remote copies, remote signals or barrier semaphores. Data moves between devices by JAX's collectives and lax.ppermute only.
A program may use at most 192 MiB of HBM per device.

```python
import jax
import jax.numpy as jnp
from jax import lax

D = 768
HEADS = 12
HEAD_DIM = 64
FF = 3072
SLOT = 512
UNIT = 128
PER_DEV = 4
SLOTS = 32
SEQS = 128


def packing_plan(key):
    slot_count = SEQS // PER_DEV
    unit_count = SLOT // UNIT
    base_key = jax.random.fold_in(key, 4099)
    cut_key, pick_key, trim_key, order_key = jax.random.split(base_key, 4)
    cut_points = jnp.sort(jax.random.randint(cut_key, (slot_count, PER_DEV - 1), 0, unit_count + 1), axis=1)
    chosen = jax.random.randint(pick_key, (), 0, slot_count)
    full_slot = (jnp.arange(slot_count) == chosen)[:, None]
    cut_points = jnp.where(full_slot, unit_count, cut_points).astype(jnp.int32)
    boundary = jnp.concatenate([jnp.zeros((slot_count, 1), jnp.int32), cut_points, jnp.full((slot_count, 1), unit_count, jnp.int32)], axis=1)
    span_units = boundary[:, 1:] - boundary[:, :-1]
    trimmed = jax.random.randint(trim_key, (slot_count, PER_DEV), 0, UNIT // 2)
    trimmed = jnp.where(full_slot, 0, trimmed)
    slot_lengths = jnp.where(span_units > 0, span_units * UNIT - trimmed, 0).reshape(-1).astype(jnp.int32)
    permuted = jax.random.permutation(order_key, SEQS).astype(jnp.int32)
    return (slot_lengths[permuted], permuted)


def draw_lengths(key, part):
    return packing_plan(key)[0]


def draw_packing(key, part):
    return packing_plan(key)[1]


def block_scale(key, extent, shards, smallest, high):
    loudness = 1.0
    for axis_at, shards_of in shards:
        steps = jax.random.uniform(jax.random.fold_in(jax.random.fold_in(key, 6), axis_at), (shards_of,), jnp.float32, smallest / len(shards), high / len(shards))
        loudness = loudness * jnp.repeat(jnp.exp(steps), extent[axis_at] // shards_of).reshape((-1,) + (1,) * (len(extent) - 1 - axis_at))
    return loudness


def noise(stream_key, dims, spread, bound, cuts=(), kind=jnp.bfloat16):
    values = spread * jax.random.normal(stream_key, dims, jnp.float32)
    if cuts:
        values = values * block_scale(stream_key, dims, cuts, -0.22, 0.18)
    return jnp.clip(values, -bound, bound).astype(kind)


def setup_inputs(seed: int = 0) -> dict:
    splits = jax.random.split(jax.random.key(seed), 18)
    return {
        "tokens": noise(splits[0], (SLOT, SLOTS, D), 1.0, 6.0, ((1, 32),)),
        "cotangent": noise(splits[1], (SLOT, SLOTS, D), 1.0, 6.0, ((1, 32),)),
        "lengths": draw_lengths(jax.random.fold_in(splits[17], 71), 0),
        "packing": draw_packing(jax.random.fold_in(splits[17], 71), 0),
        "qkv_weight": noise(splits[4], (D, 3 * D), D ** -0.5, 0.21875, ((0, 4),)),
        "query_bias": noise(splits[5], (D,), 0.5, 3.0, ((0, 4),)),
        "value_bias": noise(splits[6], (D,), 0.05, 0.29882812, ((0, 4),)),
        "out_weight": noise(splits[7], (D, D), (max(D // 64, 1)) ** -0.5, 1.75, ((0, 4),)),
        "out_bias": noise(splits[8], (D,), 0.2, 1.1953125, ((0, 4),)),
        "first_gain": jnp.clip(1.0 + 0.1 * jax.random.normal(splits[9], (D,), jnp.float32), 0.5, 1.5).astype(jnp.bfloat16),
        "first_shift": noise(splits[10], (D,), 0.2, 1.1953125, ((0, 4),)),
        "up_weight": noise(splits[11], (D, FF), D ** -0.5, 0.21875, ((0, 4),)),
        "up_bias": noise(splits[12], (FF,), 0.2, 1.1953125, ((0, 4),)),
        "down_weight": noise(splits[13], (FF, D), FF ** -0.5, 0.109375, ((0, 4),)),
        "down_bias": noise(splits[14], (D,), 0.2, 1.1953125, ((0, 4),)),
        "second_gain": jnp.clip(1.0 + 0.1 * jax.random.normal(splits[15], (D,), jnp.float32), 0.5, 1.5).astype(jnp.bfloat16),
        "second_shift": noise(splits[16], (D,), 0.2, 1.1953125, ((0, 4),)),
    }


@jax.custom_vjp
def low(v):
    return lax.optimization_barrier(v.astype(jnp.bfloat16)).astype(jnp.float32)

@jax.custom_vjp
def low_back(v):
    return v

def low_keep(v):
    return (low(v), None)

def low_pass(kept, grad):
    return (grad,)

def back_keep(v):
    return (v, None)

def back_low(kept, grad):
    return (low(grad),)
low.defvjp(low_keep, low_pass)
low_back.defvjp(back_keep, back_low)
EPS = 1e-06
MASKED = -1e+30
HIGHEST = lax.Precision.HIGHEST

def layer_norm(hidden, gain_row, shift_row):
    centre = hidden - lax.optimization_barrier(jnp.mean(hidden, axis=-1, keepdims=True))
    normal = centre * lax.rsqrt(lax.optimization_barrier(jnp.mean(centre * centre, axis=-1, keepdims=True)) + EPS)
    return normal * gain_row + shift_row

def gelu_exact(hidden):
    return 0.5 * hidden * (1.0 + lax.erf(hidden * 0.7071067811865476))

def packed_layout(lengths, packing, slot_count):
    span_rows = ((lengths + UNIT - 1) // UNIT * UNIT).astype(jnp.int32)
    loader_off = (jnp.cumsum(span_rows) - span_rows).astype(jnp.int32)
    holder = jnp.argsort(packing).astype(jnp.int32)
    span_grid = span_rows[holder].reshape(slot_count, PER_DEV)
    entry_off = (jnp.cumsum(span_grid, axis=1) - span_grid).astype(jnp.int32)
    positions = jnp.arange(SLOT, dtype=jnp.int32)
    entry_end = entry_off + span_grid
    entry_id = lax.optimization_barrier(jnp.sum((entry_end[:, None, :] <= positions[None, :, None]).astype(jnp.int32), axis=2)).astype(jnp.int32)
    seq_grid = holder.reshape(slot_count, PER_DEV)
    seq_row = jnp.take_along_axis(seq_grid, entry_id, axis=1)
    within = positions[None, :] - jnp.take_along_axis(entry_off, entry_id, axis=1)
    source = (loader_off[seq_row] + within).astype(jnp.int32)
    valid_row = within < lengths[seq_row]
    return (source, valid_row, entry_id)

def layer_slot(params, packed, valid_row, entry_id):
    qkv_weight, query_bias, value_bias, out_weight, out_bias, first_gain, first_shift, up_weight, up_bias, down_weight, down_bias, second_gain, second_shift = params
    bias_row = jnp.concatenate([query_bias, jnp.zeros_like(query_bias), value_bias])
    projected = low_back(low(jnp.dot(packed, qkv_weight, precision=HIGHEST) + bias_row))
    queries = projected[:, :D].reshape(SLOT, HEADS, HEAD_DIM)
    key_rows = projected[:, D:2 * D].reshape(SLOT, HEADS, HEAD_DIM)
    values = projected[:, 2 * D:].reshape(SLOT, HEADS, HEAD_DIM)
    scores = low_back(jnp.einsum('qhd,khd->hqk', queries, key_rows, precision=HIGHEST) * HEAD_DIM ** (-0.5))
    allowed = (entry_id[:, None] == entry_id[None, :]) & valid_row[None, :]
    scores = jnp.where(allowed[None], scores, MASKED)
    exponent = jnp.exp(scores - lax.optimization_barrier(jnp.max(scores, axis=-1, keepdims=True)))
    softmax = low(exponent / lax.optimization_barrier(jnp.sum(exponent, axis=-1, keepdims=True)))
    attended = jnp.einsum('hqk,khd->qhd', softmax, values, precision=HIGHEST).reshape(SLOT, D)
    attended = low_back(low(attended))
    branch = low_back(jnp.dot(attended, out_weight, precision=HIGHEST) + out_bias)
    normed = low(layer_norm(packed + branch, first_gain, first_shift))
    hidden_pre = low_back(jnp.dot(normed, up_weight, precision=HIGHEST) + up_bias)
    hidden_act = low(gelu_exact(hidden_pre))
    down_out = low_back(jnp.dot(hidden_act, down_weight, precision=HIGHEST) + down_bias)
    final_norm = layer_norm(normed + down_out, second_gain, second_shift)
    return final_norm * valid_row[:, None].astype(jnp.float32)

def reference(tokens, cotangent, lengths, packing, qkv_weight, query_bias, value_bias, out_weight, out_bias, first_gain, first_shift, up_weight, up_bias, down_weight, down_bias, second_gain, second_shift):
    slot_count = tokens.shape[1]
    source, valid_row, entry_id = packed_layout(lengths, packing, slot_count)
    flat_source = source.reshape(-1)
    packed = tokens.astype(jnp.float32).reshape(-1, D)[flat_source].reshape(slot_count, SLOT, D)
    grad_in = cotangent.astype(jnp.float32).reshape(-1, D)[flat_source].reshape(slot_count, SLOT, D)
    params = tuple((member.astype(jnp.float32) for member in (qkv_weight, query_bias, value_bias, out_weight, out_bias, first_gain, first_shift, up_weight, up_bias, down_weight, down_bias, second_gain, second_shift)))
    slot_step = jax.checkpoint(layer_slot)

    def forward(weights, inputs):

        def advance(running, member):
            return (running, slot_step(weights, member[0], member[1], member[2]))
        running_end, stacked = lax.scan(advance, jnp.zeros((), jnp.float32), (inputs, valid_row, entry_id))
        return stacked
    result, pullback = jax.vjp(forward, params, packed)
    grad_params, grad_packed = pullback(grad_in)
    restore = jnp.argsort(flat_source).astype(jnp.int32)
    output = result.reshape(-1, D)[restore].reshape(SLOT, slot_count, D).astype(jnp.bfloat16)
    grad_tokens = grad_packed.reshape(-1, D)[restore].reshape(SLOT, slot_count, D).astype(jnp.bfloat16)
    grad_qkv, grad_query, grad_value, grad_out_w, grad_out_b, grad_first_g, grad_first_s, grad_up_w, grad_up_b, grad_down_w, grad_down_b, grad_second_g, grad_second_s = grad_params
    return (output, grad_tokens, grad_qkv, grad_query, grad_value, grad_out_w, grad_out_b, grad_first_g, grad_first_s, grad_up_w, grad_up_b, grad_down_w, grad_down_b, grad_second_g, grad_second_s)
```

```python
import functools

import jax
import jax.numpy as jnp
from jax import lax
from jax.experimental import pallas as pl
from jax.experimental.pallas import tpu as pltpu
from jax.sharding import PartitionSpec as P

HEADS = 12
HEAD_DIM = 64
UNIT = 128
PER_DEV = 4
LANES = 128
EPS = 1e-06
MASKED = -1e30
ROOT_HALF = 0.7071067811865476
INV_ROOT_TAU = 0.3989422804014327


bf16 = jnp.bfloat16
f32 = jnp.float32


def layer_stats(hidden):
    centre = hidden - jnp.mean(hidden, axis=-1, keepdims=True)
    inv_scale = lax.rsqrt(jnp.mean(centre * centre, axis=-1, keepdims=True) + EPS)
    return (centre * inv_scale, inv_scale)


def norm_back(grad_out, normal, inv_scale, gain_row):
    grad_normal = grad_out * gain_row
    inner_sum = (
        grad_normal
        - jnp.mean(grad_normal, axis=-1, keepdims=True)
        - normal * jnp.mean(grad_normal * normal, axis=-1, keepdims=True)
    )
    return (inv_scale * inner_sum, jnp.sum(grad_out * normal, axis=0), jnp.sum(grad_out, axis=0))


def gelu_exact(hidden):
    return 0.5 * hidden * (1.0 + lax.erf(hidden * ROOT_HALF))


def gelu_slope(hidden):
    return (
        0.5 * (1.0 + lax.erf(hidden * ROOT_HALF))
        + hidden * jnp.exp(-0.5 * hidden * hidden) * INV_ROOT_TAU
    )


def times_transposed(left, right):
    return lax.dot_general(left, right, (((1,), (1,)), ((), ())), preferred_element_type=f32)


def over_rows(left, right):
    return lax.dot_general(left, right, (((0,), (0,)), ((), ())), preferred_element_type=f32)


def routing(lengths, packing, slot_count, self_index):
    span = (lengths + UNIT - 1) // UNIT
    seqs = jnp.arange(lengths.shape[0], dtype=jnp.int32)
    start = jnp.sum(jnp.where(seqs[None, :] < seqs[:, None], span[None, :], 0), axis=1)
    off = jnp.sum(jnp.where(packing[None, :] < packing[:, None], span[None, :], 0), axis=1)
    unit = jnp.arange(PER_DEV * slot_count, dtype=jnp.int32)[:, None]
    held = (off[None, :] <= unit) & (unit < (off + span)[None, :])
    to_loader = jnp.sum(jnp.where(held, start[None, :] - off[None, :] + unit, 0), axis=1)
    homed = (start[None, :] <= unit) & (unit < (start + span)[None, :])
    to_slot = jnp.sum(jnp.where(homed, off[None, :] - start[None, :] + unit, 0), axis=1)
    mine = (self_index * PER_DEV + jnp.arange(PER_DEV, dtype=jnp.int32))[:, None]
    own = (off[None, :] <= mine) & (mine < (off + span)[None, :])
    entry = jnp.sum(jnp.where(own, seqs[None, :], 0), axis=1)
    count = jnp.sum(jnp.where(own, lengths[None, :] - (mine - off[None, :]) * UNIT, 0), axis=1)
    return (to_loader, to_slot, entry, count)


def swap(value, mask, size):
    return lax.ppermute(value, "rep", [(i, i ^ mask) for i in range(size)])


def shift(value, step, size):
    return lax.ppermute(value, "shard", [(i, (i + step) % size) for i in range(size)])


def assemble(near, far, local, where, rows, columns, plane, group):
    block_rows, block_columns = near.shape[2:]
    count = plane * (group - 1)
    local_rows = local.shape[0]

    def kernel(where_ref, near_ref, far_ref, local_ref, out_ref, sems):
        spot, core, z = where_ref[0], where_ref[1], where_ref[2]
        copies = [
            pltpu.make_async_copy(
                local_ref,
                out_ref.at[pl.ds(pl.multiple_of(z * local_rows, local_rows), local_rows), :],
                sems.at[0],
            )
        ]
        for mask in range(plane):
            for step in range(1, group):
                row = lax.rem(z + group - step, group) * local_rows + (spot ^ mask) * block_rows
                row = pl.multiple_of(row, block_rows)
                for side, ref in enumerate((near_ref, far_ref)):
                    column = pl.multiple_of((core ^ side) * block_columns, LANES)
                    copies.append(
                        pltpu.make_async_copy(
                            ref.at[mask, step - 1],
                            out_ref.at[pl.ds(row, block_rows), pl.ds(column, block_columns)],
                            sems.at[len(copies)],
                        )
                    )
        for copy in copies:
            copy.start()
        for copy in copies:
            copy.wait()

    return pl.pallas_call(
        kernel,
        out_shape=jax.ShapeDtypeStruct((rows, columns), near.dtype),
        in_specs=[pl.BlockSpec(memory_space=pltpu.SMEM)] + [pl.BlockSpec(memory_space=pl.ANY)] * 3,
        out_specs=pl.BlockSpec(memory_space=pltpu.VMEM),
        scratch_shapes=[pltpu.SemaphoreType.DMA((2 * count + 1,))],
        compiler_params=pltpu.CompilerParams(vmem_limit_bytes=rows * columns * 2 + (4 << 20)),
        cost_estimate=pl.CostEstimate(
            flops=0, bytes_accessed=4 * rows * columns, transcendentals=0
        ),
    )(where, near, far, local)


def assemble_plain(near, far, local, where, rows, columns, plane, group):
    block_rows, block_columns = near.shape[2:]
    local_rows = local.shape[0]
    spot, core, z = where[0], where[1], where[2]
    out = jnp.zeros((rows, columns), near.dtype)
    out = lax.dynamic_update_slice(out, local, (z * local_rows, 0))
    for mask in range(plane):
        for step in range(1, group):
            row = lax.rem(z + group - step, group) * local_rows + (spot ^ mask) * block_rows
            for side, block in enumerate((near, far)):
                out = lax.dynamic_update_slice(
                    out, block[mask, step - 1], (row, (core ^ side) * block_columns)
                )
    return out


def gather_plane(value, masks):
    size = 2 * (1 << len(masks))
    parts, labels = [value], [0]
    for mask in masks:
        held = parts[0][None] if len(parts) == 1 and parts[0].ndim == value.ndim else parts[0]
        held = jnp.concatenate([held, swap(held, mask, size)], axis=0)
        parts, labels = [held], labels + [label ^ mask for label in labels]
    order = [labels.index(mask << 1) for mask in range(size // 2)]
    held = parts[0]
    if order != sorted(order):
        held = jnp.stack([held[i] for i in order])
    return held


def gather_weight(locals_, masks, where, plane, group):
    spot, core = where[0], where[1]
    size = 2 * plane
    blocks = []
    for member in locals_:
        rows, columns = member.shape[0] // plane, member.shape[1] // 2
        blocks.append(
            lax.dynamic_slice(member, (spot * rows, core * columns), (rows, columns))
        )
    widths = [block.shape[1] for block in blocks]
    pack = jnp.concatenate(blocks, axis=1) if len(blocks) > 1 else blocks[0]
    foreign = jnp.stack([shift(pack, step, group) for step in range(1, group)])
    near = gather_plane(foreign, masks)
    far = swap(near, 1, size)
    out, begin = [], 0
    for member, width in zip(locals_, widths):
        rows, columns = member.shape[0] * group, member.shape[1]
        aligned = (member.shape[0] // plane) % 16 == 0
        place = assemble if aligned else assemble_plain
        out.append(
            place(
                near[..., begin : begin + width],
                far[..., begin : begin + width],
                member,
                where,
                rows,
                columns,
                plane,
                group,
            )
        )
        begin += width
    return out


def reduce_weight(left, right, masks, where, plane, group):
    spot, core, z = where[0], where[1], where[2]
    size = 2 * plane
    columns = right.shape[1] // 2
    other = lax.dynamic_slice_in_dim(right, (1 - core) * columns, columns, 1)
    own = lax.dynamic_slice_in_dim(right, core * columns, columns, 1)
    got = swap(over_rows(left, other).astype(bf16), 1, size)
    chip = (over_rows(left, own) + got.astype(f32)).astype(bf16)
    local_rows = left.shape[1] // group
    block_rows = local_rows // plane
    bits = plane.bit_length() - 1
    held = chip.reshape((group,) + (2,) * bits + (block_rows, columns))
    axes = [1 << (bits - 1 - i) for i in range(bits)]
    for mask in masks:
        at = 1 + axes.index(mask >> 1)
        bit = (spot // (mask >> 1)) % 2
        away = lax.dynamic_index_in_dim(held, 1 - bit, at, keepdims=False)
        kept = lax.dynamic_index_in_dim(held, bit, at, keepdims=False)
        held = (kept.astype(f32) + swap(away, mask, size).astype(f32)).astype(bf16)
        axes.remove(mask >> 1)
    total = lax.dynamic_index_in_dim(held, z, 0, keepdims=False).astype(f32)
    for step in range(1, group):
        block = lax.dynamic_index_in_dim(held, (z + step) % group, 0, keepdims=False)
        total = total + shift(block, step, group).astype(f32)
    near = gather_plane(total.astype(bf16), masks)
    far = swap(near, 1, size)
    out = jnp.zeros((local_rows, 2 * columns), f32)
    both = jnp.stack([near, far], axis=0)
    natural = jnp.stack(
        [
            jnp.stack(
                [
                    lax.dynamic_index_in_dim(
                        lax.dynamic_index_in_dim(both, core ^ side, 0, keepdims=False),
                        spot ^ mask,
                        0,
                        keepdims=False,
                    )
                    for side in range(2)
                ],
                axis=1,
            )
            for mask in range(plane)
        ]
    )
    return natural.reshape(local_rows, 2 * columns).astype(f32)


def sum_small(vector, rep_size, group):
    mask = 1
    while mask < rep_size:
        vector = vector + swap(vector, mask, rep_size)
        mask *= 2
    total = vector
    for step in range(1, group):
        total = total + shift(vector, step, group)
    return total


def per_device(
    tokens,
    cotangent,
    lengths,
    packing,
    qkv_weight,
    query_bias,
    value_bias,
    out_weight,
    out_bias,
    first_gain,
    first_shift,
    up_weight,
    up_bias,
    down_weight,
    down_bias,
    second_gain,
    second_shift,
):
    both_axes = ("rep", "shard")
    slot_count = lax.axis_size(both_axes)
    self_index = lax.axis_index(both_axes)
    rep_size, group = lax.axis_size("rep"), lax.axis_size("shard")
    plane = rep_size // 2
    rep, z = lax.axis_index("rep"), lax.axis_index("shard")
    spot, core = rep // 2, rep % 2
    where = jnp.stack([spot, core, z]).astype(jnp.int32)
    rising = [1 << (i + 1) for i in range(plane.bit_length() - 1)]
    falling = rising[::-1]
    row_count, _, model_width = tokens.shape
    share = row_count // slot_count
    share_unit = share // PER_DEV

    to_loader, to_slot, entry, count = routing(lengths, packing, slot_count, self_index)

    def to_slots(rows):
        sent = rows.reshape(row_count // share_unit, share_unit, model_width)[to_loader]
        sent = sent.reshape(slot_count, share, model_width)
        return lax.all_to_all(sent, both_axes, split_axis=0, concat_axis=0, tiled=True).reshape(
            row_count, model_width
        )

    def to_home(rows):
        got = lax.all_to_all(
            rows.reshape(slot_count, share, model_width),
            both_axes,
            split_axis=0,
            concat_axis=0,
            tiled=True,
        )
        got = got.reshape(row_count // share_unit, share_unit, model_width)[to_slot]
        return got.reshape(row_count, 1, model_width)

    row = jnp.arange(row_count, dtype=jnp.int32)
    row_unit = row // share_unit % PER_DEV
    row_place = row % share_unit * slot_count + row // share
    picked = row_unit[:, None] == jnp.arange(PER_DEV, dtype=jnp.int32)[None, :]
    entry_id = jnp.sum(jnp.where(picked, entry[None, :], 0), axis=1)
    valid_row = row_place < jnp.sum(jnp.where(picked, count[None, :], 0), axis=1)
    row_mask = valid_row.astype(f32)[:, None]

    packed = to_slots(tokens)
    small = jnp.concatenate(
        [
            query_bias,
            value_bias,
            out_bias,
            first_gain,
            first_shift,
            down_bias,
            second_gain,
            second_shift,
            up_bias,
        ]
    )[None]
    smalls = jnp.zeros((group, small.shape[1]), bf16)
    smalls = lax.dynamic_update_slice(smalls, small, (z, 0))
    for step in range(1, group):
        smalls = lax.dynamic_update_slice(
            smalls, shift(small, step, group), ((z + group - step) % group, 0)
        )
    smalls = smalls.astype(f32)
    part = query_bias.shape[0]
    (
        whole_query_bias,
        whole_value_bias,
        whole_out_bias,
        whole_first_gain,
        whole_first_shift,
        whole_down_bias,
        whole_second_gain,
        whole_second_shift,
    ) = [smalls[:, i * part : (i + 1) * part].reshape(-1) for i in range(8)]
    whole_up_bias = smalls[:, 8 * part :].reshape(-1)

    (whole_qkv,) = gather_weight([qkv_weight], rising, where, plane, group)
    grad_final = to_slots(cotangent).astype(f32) * row_mask
    whole_up, whole_out = gather_weight([up_weight, out_weight], falling, where, plane, group)
    (whole_down,) = gather_weight([down_weight], rising, where, plane, group)

    score_scale = HEAD_DIM ** (-0.5)
    bias_row = jnp.concatenate(
        [whole_query_bias, jnp.zeros_like(whole_query_bias), whole_value_bias]
    )
    projected = (jnp.dot(packed, whole_qkv, preferred_element_type=f32) + bias_row).astype(bf16)
    queries = projected[:, :model_width].reshape(row_count, HEADS, HEAD_DIM)
    key_rows = projected[:, model_width : 2 * model_width].reshape(row_count, HEADS, HEAD_DIM)
    values = projected[:, 2 * model_width :].reshape(row_count, HEADS, HEAD_DIM)

    allowed = (entry_id[:, None] == entry_id[None, :]) & valid_row[None, :]

    def block_scores():
        raw = jnp.einsum("qhd,khd->hqk", queries, key_rows, preferred_element_type=f32)
        return jnp.where(allowed[None], raw * score_scale, MASKED)

    scores = block_scores()
    row_max = jnp.max(scores, axis=-1, keepdims=True)
    exponent = jnp.exp(scores - row_max)
    row_total = jnp.sum(exponent, axis=-1, keepdims=True)
    softmax_low = (exponent / row_total).astype(bf16)
    attended = (
        jnp.einsum("hqk,khd->qhd", softmax_low, values, preferred_element_type=f32)
        .astype(bf16)
        .reshape(row_count, model_width)
    )
    log_total = row_max + jnp.log(row_total)
    branch = jnp.dot(attended, whole_out, preferred_element_type=f32) + whole_out_bias
    first_normal, first_scale = layer_stats(packed.astype(f32) + branch)
    normed = (first_normal * whole_first_gain + whole_first_shift).astype(bf16)
    hidden_pre = jnp.dot(normed, whole_up, preferred_element_type=f32) + whole_up_bias
    hidden_act = gelu_exact(hidden_pre).astype(bf16)
    down_out = jnp.dot(hidden_act, whole_down, preferred_element_type=f32) + whole_down_bias
    second_normal, second_scale = layer_stats(normed.astype(f32) + down_out)
    final_norm = (second_normal * whole_second_gain + whole_second_shift) * row_mask
    output = to_home(final_norm.astype(bf16))

    grad_mid, grad_second_gain, grad_second_shift = norm_back(
        grad_final, second_normal, second_scale, whole_second_gain
    )
    grad_down = grad_mid.astype(bf16)
    reduced_down = reduce_weight(hidden_act, grad_down, rising, where, plane, group)
    grad_down_bias = jnp.sum(grad_down.astype(f32), axis=0)
    grad_pre = (times_transposed(grad_down, whole_down) * gelu_slope(hidden_pre)).astype(bf16)
    reduced_up = reduce_weight(normed, grad_pre, falling, where, plane, group)
    grad_up_bias = jnp.sum(grad_pre.astype(f32), axis=0)
    grad_normed = grad_mid + times_transposed(grad_pre, whole_up)
    grad_res, grad_first_gain, grad_first_shift = norm_back(
        grad_normed, first_normal, first_scale, whole_first_gain
    )
    grad_branch = grad_res.astype(bf16)
    reduced_out = reduce_weight(attended, grad_branch, falling, where, plane, group)
    grad_out_bias = jnp.sum(grad_branch.astype(f32), axis=0)
    grad_attended = (
        times_transposed(grad_branch, whole_out)
        .astype(bf16)
        .reshape(row_count, HEADS, HEAD_DIM)
    )
    softmax = jnp.exp(block_scores() - log_total)
    grad_values = jnp.einsum(
        "hqk,qhd->khd", softmax.astype(bf16), grad_attended, preferred_element_type=f32
    )
    grad_probs = jnp.einsum("qhd,khd->hqk", grad_attended, values, preferred_element_type=f32)
    inner_sum = jnp.sum(softmax * grad_probs, axis=-1, keepdims=True)
    grad_scores = (softmax * (grad_probs - inner_sum)).astype(bf16)
    grad_queries = score_scale * jnp.einsum(
        "hqk,khd->qhd", grad_scores, key_rows, preferred_element_type=f32
    )
    grad_keys = score_scale * jnp.einsum(
        "hqk,qhd->khd", grad_scores, queries, preferred_element_type=f32
    )
    grad_projected = jnp.concatenate(
        [
            grad_queries.reshape(row_count, model_width),
            grad_keys.reshape(row_count, model_width),
            grad_values.reshape(row_count, model_width),
        ],
        axis=1,
    ).astype(bf16)
    reduced_qkv = reduce_weight(packed, grad_projected, rising, where, plane, group)
    column_sums = jnp.sum(grad_projected.astype(f32), axis=0)
    grad_input = (grad_res + times_transposed(grad_projected, whole_qkv)).astype(bf16)
    grad_tokens = to_home(grad_input)

    vectors = [
        column_sums[:model_width],
        column_sums[2 * model_width :],
        grad_out_bias,
        grad_first_gain,
        grad_first_shift,
        grad_down_bias,
        grad_second_gain,
        grad_second_shift,
        grad_up_bias,
    ]
    summed = sum_small(
        jnp.concatenate([v.reshape(group, -1) for v in vectors], axis=1), rep_size, group
    )
    summed = lax.dynamic_index_in_dim(summed, z, 0, keepdims=False)
    own = [summed[i * part : (i + 1) * part] for i in range(8)]
    own_up_bias = summed[8 * part :]
    return (
        output,
        grad_tokens,
        reduced_qkv,
        own[0],
        own[1],
        reduced_out,
        own[2],
        own[3],
        own[4],
        reduced_up,
        own_up_bias,
        reduced_down,
        own[5],
        own[6],
        own[7],
    )


def solution(mesh):
    tokens = P(None, ("rep", "shard"), None)
    matrix, vector = P("shard", None), P("shard")
    in_specs = (
        tokens,
        tokens,
        P(),
        P(),
        matrix,
        vector,
        vector,
        matrix,
        vector,
        vector,
        vector,
        matrix,
        vector,
        matrix,
        vector,
        vector,
        vector,
    )
    out_specs = (
        tokens,
        tokens,
        matrix,
        vector,
        vector,
        matrix,
        vector,
        vector,
        vector,
        matrix,
        vector,
        matrix,
        vector,
        vector,
        vector,
    )
    return jax.shard_map(
        per_device, mesh=mesh, in_specs=in_specs, out_specs=out_specs, check_vma=False
    )
```
